512 devices in a mesh: dp: 64 (over y_hi, z, core), seq: 8 (over x, y_lo).
Axes of the slice: x: 4, y: 4 (y_hi: 2, y_lo: 2; y = y_hi * 2 + y_lo), z: 16, core: 2. Of those that a mesh axis runs over, the one named last changes fastest.
Arguments:
- queries: bfloat16 [65536, 4096], P(('dp', 'seq')), may hold values from -180 to 180, as said below
- keys: bfloat16 [65536, 512], P(('dp', 'seq')), may hold values from -6 to 6, as said below
- values: bfloat16 [65536, 512], P(('dp', 'seq')), may hold values from -6 to 6
- lengths: int32 [64, 16], P('dp'), may hold values from 1 to 512, 1024 in all within a row
- out_grad: bfloat16 [65536, 4096], P(('dp', 'seq')), may hold values from -6 to 6
Outputs:
- attended: bfloat16 [65536, 4096], P(('dp', 'seq'))
- query_grad: bfloat16 [65536, 4096], P(('dp', 'seq'))
- key_grad: bfloat16 [65536, 512], P(('dp', 'seq'))
- value_grad: bfloat16 [65536, 512], P(('dp', 'seq'))
The draws below stay inside these ranges and needn't reach their ends.
Inputs may be any that keep to these rules, and one draw needn't show every extreme that they name: `queries`: queries stay within this range. `keys`: keys stay within this range.
All inputs are finite; a program needn't handle non-finite values.
Results may differ from the reference program's by a relative error of at most 0.0095.
Values may be sent and summed in bfloat16 or wider, within the bound.
No kernel may reach another device: no remote copies, remote signals or barrier semaphores. Data moves between devices by JAX's collectives and lax.ppermute only.
A program may use at most 64 MiB of HBM per device.

```python
import math
import jax
import jax.numpy as jnp
import numpy as np
from jax import lax

H = 32
KVH = 4
HD = 128
GROUP = 8
SEGS = 16
LEN = 1024
MOST = 512
BATCH_TOK = 65536
N_DP = 64
N_SEQ = 8


def draw_pair(key):
    base_q = jnp.clip(jax.random.normal(jax.random.fold_in(key, 11), (BATCH_TOK, KVH, GROUP, HD), jnp.float32), -6.0, 6.0)
    base_k = jnp.clip(jax.random.normal(jax.random.fold_in(key, 12), (BATCH_TOK, KVH, HD), jnp.float32), -6.0, 6.0)
    return (base_q.reshape(BATCH_TOK, H * HD), base_k.reshape(BATCH_TOK, KVH * HD))


def draw_queries(key, part):
    return draw_pair(key)[0].astype(jnp.bfloat16)


def draw_keys(key, part):
    return draw_pair(key)[1].astype(jnp.bfloat16)


def block_levels(key, extent, pieces, low, top_value):
    factor_of, own = 1.0, jax.random.fold_in(key, 6)
    for position, parts in pieces:
        heights = jnp.exp(jax.random.uniform(jax.random.fold_in(own, position), (parts,), jnp.float32, low / len(pieces), top_value / len(pieces)))
        factor_of = factor_of * jnp.repeat(heights, extent[position] // parts).reshape([-1 if axis == position else 1 for axis in range(len(extent))])
    return factor_of


def profile(count, total, reach, lean):
    weights = [(1 << 20) // math.isqrt(grade ** lean) + 1 for grade in range(2, count + 1)]
    spare, given = total - reach - (count - 1), [1] * (count - 1)
    while spare > 0:
        free = [i for i in range(count - 1) if given[i] < reach]
        pool, budget = sum([weights[i] for i in free]), spare
        for i in free:
            more = min(reach - given[i], max(1, budget * weights[i] // pool), spare)
            given[i] = given[i] + more
            spare = spare - more
    return np.array([reach] + given)


def uneven(stream_key, count, total, reach, slope):
    if count == 2:
        one = jax.random.randint(stream_key, (), max(1, total - reach), min(reach, total - 1) + 1)
        return jnp.stack([one, total - one])
    tallies = jnp.asarray(profile(count, total, reach, slope), jnp.int32)
    twos = (count - 1) // 2
    donor, sink = tallies[1:1 + 2 * twos:2], tallies[2:2 + 2 * twos:2]
    room = jnp.minimum(donor - 1, reach - sink)
    passed = jax.random.randint(jax.random.fold_in(stream_key, 1), (twos,), 0, 1 << 20) % (room + 1)
    tallies = tallies.at[1:1 + 2 * twos:2].set(donor - passed).at[2:2 + 2 * twos:2].set(sink + passed)
    return tallies[jax.random.permutation(jax.random.fold_in(stream_key, 2), count)]


def centred(own_key, dims, deviation, bound, cuts=(), held_as=jnp.bfloat16):
    result = jax.random.normal(own_key, dims, jnp.float32) * deviation
    if len(cuts) > 0:
        result = block_levels(own_key, dims, cuts, -0.22, 0.18) * result
    return jnp.clip(result, min=-bound, max=bound).astype(held_as)


def setup_inputs(seed: int = 0) -> dict:
    seeds = jax.random.split(jax.random.key(seed), 6)
    queries = draw_queries(jax.random.fold_in(seeds[5], 71), 0)
    keys = draw_keys(jax.random.fold_in(seeds[5], 71), 0)
    values = centred(seeds[2], (BATCH_TOK, KVH * HD), 1.0, 6.0, ((0, 512),))
    lengths = jax.vmap(lambda own: uneven(own, SEGS, LEN, MOST, 2))(jax.random.split(seeds[3], N_DP)).reshape((N_DP, SEGS)).astype(jnp.int32)
    out_grad = centred(seeds[4], (BATCH_TOK, H * HD), 1.0, 6.0, ((0, 512),))
    return dict(queries=queries, keys=keys, values=values, lengths=lengths, out_grad=out_grad)


def doc_of(pos, ends):
    return jnp.sum((pos[:, None] >= ends[None, :]).astype(jnp.int32), axis=1)


def one_sequence(args):
    queries, keys, values, lens, out_grad = args
    scale = HD ** -0.5
    qh = queries.astype(jnp.float32).reshape(LEN, KVH, GROUP, HD)
    kh = keys.astype(jnp.float32).reshape(LEN, KVH, HD)
    vh = values.astype(jnp.float32).reshape(LEN, KVH, HD)
    gh = out_grad.astype(jnp.float32).reshape(LEN, KVH, GROUP, HD)
    ends = jnp.cumsum(lens).astype(jnp.int32)
    pos = jnp.arange(LEN, dtype=jnp.int32)
    docs = doc_of(pos, ends)
    visible = (docs[:, None] == docs[None, :]) & (pos[None, :] <= pos[:, None])
    scores = jnp.einsum('tkgd,skd->kgts', qh, kh) * scale
    scores = jnp.where(visible, scores, -1e30)
    top = jnp.max(scores, axis=-1)
    expo = jnp.where(visible, jnp.exp(scores - top[..., None]), 0.0)
    lsum = jnp.sum(expo, axis=-1)
    weights = lax.optimization_barrier(expo.astype(jnp.bfloat16)).astype(jnp.float32)
    heads_out = jnp.einsum('kgts,skd->kgtd', weights, vh) / lsum[..., None]
    attended = heads_out.transpose(2, 0, 1, 3).reshape(LEN, H * HD).astype(jnp.bfloat16)
    rowdot = jnp.sum(gh * attended.astype(jnp.float32).reshape(LEN, KVH, GROUP, HD), axis=-1).transpose(1, 2, 0)
    probs = expo / lsum[..., None]
    probs_b = lax.optimization_barrier(probs.astype(jnp.bfloat16)).astype(jnp.float32)
    dprobs = jnp.einsum('tkgd,skd->kgts', gh, vh)
    dscores = lax.optimization_barrier((probs * (dprobs - rowdot[..., None])).astype(jnp.bfloat16)).astype(jnp.float32)
    query_grad = (jnp.einsum('kgts,skd->kgtd', dscores, kh) * scale).transpose(2, 0, 1, 3).reshape(LEN, H * HD).astype(jnp.bfloat16)
    runs = LEN // N_SEQ
    ds_runs = dscores.reshape(KVH, GROUP, N_SEQ, runs, LEN)
    pb_runs = probs_b.reshape(KVH, GROUP, N_SEQ, runs, LEN)
    q_runs = qh.reshape(N_SEQ, runs, KVH, GROUP, HD)
    g_runs = gh.reshape(N_SEQ, runs, KVH, GROUP, HD)
    key_parts = (jnp.einsum('kgjts,jtkgd->jskd', ds_runs, q_runs) * scale).astype(jnp.bfloat16).astype(jnp.float32)
    value_parts = jnp.einsum('kgjts,jtkgd->jskd', pb_runs, g_runs).astype(jnp.bfloat16).astype(jnp.float32)
    key_grad = jnp.sum(key_parts, axis=0).reshape(LEN, KVH * HD).astype(jnp.bfloat16)
    value_grad = jnp.sum(value_parts, axis=0).reshape(LEN, KVH * HD).astype(jnp.bfloat16)
    return attended, query_grad, key_grad, value_grad


def reference(queries, keys, values, lengths, out_grad):
    split = (queries.reshape(N_DP, LEN, H * HD), keys.reshape(N_DP, LEN, KVH * HD),
             values.reshape(N_DP, LEN, KVH * HD), lengths, out_grad.reshape(N_DP, LEN, H * HD))
    attended, query_grad, key_grad, value_grad = lax.map(one_sequence, split)
    return (attended.reshape(BATCH_TOK, H * HD), query_grad.reshape(BATCH_TOK, H * HD),
            key_grad.reshape(BATCH_TOK, KVH * HD), value_grad.reshape(BATCH_TOK, KVH * HD))
```

```python
import functools

import jax
import jax.numpy as jnp
from jax import lax
from jax.experimental import pallas as pl
from jax.experimental.pallas import tpu as pltpu
from jax.sharding import PartitionSpec as P

H = 32
KVH = 4
HD = 128
GROUP = 8
SEGS = 16
MOST = 512
SCALE = HD**-0.5
EXP2_SCALE = SCALE * 1.4426950408889634
NEG = -1e30
ROWS = 128
HEADS_AT_ONCE = 4

NT = (((1,), (1,)), ((), ()))
TN = (((0,), (0,)), ((), ()))


def dot(a, b, dims=(((1,), (0,)), ((), ()))):
    return lax.dot_general(a, b, dims, preferred_element_type=jnp.float32)


def attend(chunks, lens_ref, where_ref, q_ref, g_ref, *refs):
    k_refs, v_refs = refs[:chunks], refs[chunks : 2 * chunks]
    att_ref, dq_ref = refs[2 * chunks : 2 * chunks + 2]
    part_refs = refs[2 * chunks + 2 : 3 * chunks + 2]
    bias_ref, dk_ref, dv_ref = refs[3 * chunks + 2 :]
    keys_n = chunks * ROWS

    @pl.when(pl.program_id(0) == 0)
    def _():
        run = where_ref[0]
        pos = run * ROWS + lax.broadcasted_iota(jnp.int32, (ROWS, ROWS), 0)
        lane = lax.broadcasted_iota(jnp.int32, (ROWS, ROWS), 1)
        start = jnp.zeros((ROWS, ROWS), jnp.int32)
        end = jnp.int32(0)
        for d in range(SEGS):
            end = end + lens_ref[d]
            start = jnp.where(pos >= end, end, start)
        for c in range(chunks):
            key_pos = (run - c) * ROWS + lane
            seen = (key_pos >= start) & (key_pos <= pos)
            bias_ref[:, c * ROWS : (c + 1) * ROWS] = jnp.where(seen, 0.0, NEG)

    k = jnp.concatenate([r[...] for r in k_refs], axis=0)
    v = jnp.concatenate([r[...] for r in v_refs], axis=0)
    ones = jnp.ones((keys_n, HD), jnp.bfloat16)
    v_one = jnp.concatenate([v, ones], axis=1)
    bias = bias_ref[...]
    many = HEADS_AT_ONCE
    for first in range(0, GROUP, many):
        heads = [slice(h * HD, (h + 1) * HD) for h in range(first, first + many)]
        q = jnp.concatenate([q_ref[:, h] for h in heads], axis=0)
        g = jnp.concatenate([g_ref[:, h] for h in heads], axis=0).astype(jnp.float32)
        scores = dot(q, k, NT) + jnp.concatenate([bias] * many, axis=0)
        top = jnp.max(scores, axis=1, keepdims=True)
        expo = jnp.exp2((scores - top) * EXP2_SCALE)
        weights = expo.astype(jnp.bfloat16)
        out = dot(weights, v_one)
        inv = 1.0 / out[:, HD:]
        att = (out[:, :HD] * inv).astype(jnp.bfloat16)
        rowdot = jnp.sum(g * att.astype(jnp.float32) * inv, axis=1, keepdims=True)
        g_scaled = (g * inv).astype(jnp.bfloat16)
        dprobs = dot(g_scaled, v, NT)
        dscores = (expo * (dprobs - rowdot)).astype(jnp.bfloat16)
        dq = (dot(dscores, k) * SCALE).astype(jnp.bfloat16)
        for i, h in enumerate(heads):
            att_ref[:, h] = att[i * ROWS : (i + 1) * ROWS]
            dq_ref[:, h] = dq[i * ROWS : (i + 1) * ROWS]
        dk, dv = dot(q, dscores, TN), dot(g_scaled, weights, TN)
        if first == 0:
            dk_ref[...], dv_ref[...] = dk, dv
        else:
            dk_ref[...] += dk
            dv_ref[...] += dv
    for c in range(chunks):
        cols = slice(c * ROWS, (c + 1) * ROWS)
        part_refs[c][0, 0] = (dk_ref[:, cols] * SCALE).astype(jnp.bfloat16)
        part_refs[c][0, 1] = dv_ref[:, cols].astype(jnp.bfloat16)


def total(*refs):
    part_refs, (dk_ref, dv_ref) = refs[:-2], refs[-2:]
    for h in range(KVH):
        for i, o_ref in enumerate((dk_ref, dv_ref)):
            s = part_refs[0][h, i].astype(jnp.float32)
            for r in part_refs[1:]:
                s = s + r[h, i].astype(jnp.float32)
            o_ref[:, h * HD : (h + 1) * HD] = s.T.astype(jnp.bfloat16)


def shards(queries, keys, values, lengths, out_grad):
    n = lax.axis_size("seq")
    back = min(n - 1, -(-(MOST - 1) // ROWS))
    chunks = back + 1
    run = lax.axis_index("seq").astype(jnp.int32)
    both = jnp.concatenate([keys, values], axis=1)
    got = [
        lax.ppermute(both, "seq", [(i, i + c) for i in range(n - c)])
        for c in range(1, chunks)
    ]
    wide = pl.BlockSpec((ROWS, GROUP * HD), lambda h, *_: (0, h))
    k_spec = pl.BlockSpec((ROWS, HD), lambda h, *_: (0, h))
    v_spec = pl.BlockSpec((ROWS, HD), lambda h, *_: (0, KVH + h))
    part = pl.BlockSpec((1, 2, HD, ROWS), lambda h, *_: (h, 0, 0, 0))
    part_shape = jax.ShapeDtypeStruct((KVH, 2, HD, ROWS), jnp.bfloat16)
    big = jax.ShapeDtypeStruct((ROWS, H * HD), jnp.bfloat16)
    att, dq, *parts = pl.pallas_call(
        functools.partial(attend, chunks),
        grid_spec=pltpu.PrefetchScalarGridSpec(
            num_scalar_prefetch=2,
            grid=(KVH,),
            in_specs=[wide, wide]
            + [k_spec] * chunks
            + [k_spec]
            + [v_spec] * back,
            out_specs=[wide, wide] + [part] * chunks,
            scratch_shapes=[
                pltpu.VMEM((ROWS, chunks * ROWS), jnp.float32),
                pltpu.VMEM((HD, chunks * ROWS), jnp.float32),
                pltpu.VMEM((HD, chunks * ROWS), jnp.float32),
            ],
        ),
        out_shape=[big, big] + [part_shape] * chunks,
        name="attend",
    )(lengths[0], run[None], queries, out_grad, keys, *got, values, *got)
    sent = [
        lax.ppermute(parts[c], "seq", [(i, i - c) for i in range(c, n)])
        for c in range(1, chunks)
    ]
    small = jax.ShapeDtypeStruct((ROWS, KVH * HD), jnp.bfloat16)
    dk, dv = pl.pallas_call(total, out_shape=[small, small], name="total")(
        parts[0], *sent
    )
    return att, dq, dk, dv


def solution(mesh):
    rows = P(("dp", "seq"), None)
    return jax.shard_map(
        shards,
        mesh=mesh,
        in_specs=(rows, rows, rows, P("dp", None), rows),
        out_specs=(rows,) * 4,
        check_vma=False,
    )
```

```python
import functools

import jax
import jax.numpy as jnp
from jax import lax
from jax.experimental import pallas as pl
from jax.experimental.pallas import tpu as pltpu
from jax.sharding import PartitionSpec as P


H = 32
KVH = 4
HD = 128
GROUP = 8
SEGS = 16
MOST = 512
SCALE = HD**-0.5
EXP2_SCALE = SCALE * 1.4426950408889634
NEG = -1e30
ROWS = 128
HEADS_AT_ONCE = 2
SIZES = (1, 2, 3, 4)
PIECES = 2
IN_PIECES = 2

NT = (((1,), (1,)), ((), ()))
TN = (((0,), (0,)), ((), ()))


def dot(a, b, dims=(((1,), (0,)), ((), ()))):
    return lax.dot_general(a, b, dims, preferred_element_type=jnp.float32)


def halves(a, b):
    n = a.shape[0] // 2
    return jnp.concatenate([dot(a[:n], b), dot(a[n:], b)], axis=0)


def stack(parts):
    return jnp.concatenate(parts, axis=0)


def attend(chunks, given, lens_ref, where_ref, q_ref, g_ref, *refs):
    refs = refs[given:]
    k_refs, v_refs = refs[:chunks], refs[chunks : 2 * chunks]
    att_ref, dq_ref = refs[2 * chunks : 2 * chunks + 2]
    part_refs = refs[2 * chunks + 2 : 3 * chunks + 2]
    (bias_ref,) = refs[3 * chunks + 2 :]
    run = where_ref[0]
    ends = []
    for d in range(SEGS):
        ends.append(lens_ref[d] + (ends[-1] if d else 0))

    @pl.when(pl.program_id(0) == 0)
    def _():
        pos = run * ROWS + lax.broadcasted_iota(jnp.int32, (ROWS, ROWS), 0)
        lane = lax.broadcasted_iota(jnp.int32, (ROWS, ROWS), 1)
        start = jnp.zeros((ROWS, ROWS), jnp.int32)
        for end in ends:
            start = jnp.where(pos >= end, end, start)
        for c in range(chunks):
            key_pos = (run - c) * ROWS + lane
            seen = (key_pos >= start) & (key_pos <= pos)
            bias_ref[:, c * ROWS : (c + 1) * ROWS] = jnp.where(seen, 0.0, NEG)

    first = jnp.int32(0)
    for end in ends:
        first = jnp.where(run * ROWS >= end, end, first)
    live = run - first // ROWS + 1

    def work(n):
        k = stack([r[...] for r in k_refs[:n]])
        v = stack([r[...] for r in v_refs[:n]])
        v_one = jnp.concatenate([v, jnp.ones((n * ROWS, HD), jnp.bfloat16)], axis=1)
        bias = stack([bias_ref[:, : n * ROWS]] * HEADS_AT_ONCE)
        blocks = range(GROUP // HEADS_AT_ONCE)
        heads = [
            [slice(h * HD, (h + 1) * HD) for h in range(b, b + HEADS_AT_ONCE)]
            for b in range(0, GROUP, HEADS_AT_ONCE)
        ]
        q = [stack([q_ref[:, h] for h in heads[b]]) for b in blocks]
        g = [stack([g_ref[:, h] for h in heads[b]]) for b in blocks]
        expo, weights, g_scaled, rowdot, dscores = ([] for _ in range(5))
        scores = [dot(q[b], k, NT) + bias for b in blocks]
        for b in blocks:
            top = jnp.max(scores[b], axis=1, keepdims=True)
            expo.append(jnp.exp2((scores[b] - top) * EXP2_SCALE))
            weights.append(expo[b].astype(jnp.bfloat16))
        for b in blocks:
            out = halves(weights[b], v_one)
            inv = 1.0 / out[:, HD:]
            att = (out[:, :HD] * inv).astype(jnp.bfloat16)
            wide = g[b].astype(jnp.float32) * inv
            dots = jnp.sum(wide * att.astype(jnp.float32), axis=1, keepdims=True)
            rowdot.append(dots)
            g_scaled.append(wide.astype(jnp.bfloat16))
            for i, h in enumerate(heads[b]):
                att_ref[:, h] = att[i * ROWS : (i + 1) * ROWS]
        for b in blocks:
            dprobs = dot(g_scaled[b], v, NT)
            dscores.append((expo[b] * (dprobs - rowdot[b])).astype(jnp.bfloat16))
        for b in blocks:
            dq = (halves(dscores[b], k) * SCALE).astype(jnp.bfloat16)
            for i, h in enumerate(heads[b]):
                dq_ref[:, h] = dq[i * ROWS : (i + 1) * ROWS]
        dk = dot(stack(q), stack(dscores), TN) * SCALE
        dv = dot(stack(g_scaled), stack(weights), TN)
        for c in range(n):
            cols = slice(c * ROWS, (c + 1) * ROWS)
            part_refs[c][0, 0] = dk[:, cols].astype(jnp.bfloat16)
            part_refs[c][0, 1] = dv[:, cols].astype(jnp.bfloat16)
        for c in range(n, chunks):
            part_refs[c][...] = jnp.zeros_like(part_refs[c])

    sizes = [n for n in SIZES if n < chunks] + [chunks]
    for low, n in zip([0] + sizes, sizes):
        pl.when((live > low) & (live <= n))(functools.partial(work, n))


def total(chunks, *refs):
    part_refs, o_refs = refs[:chunks], refs[-2:]
    for i, o_ref in enumerate(o_refs):
        s = part_refs[0][0, i].astype(jnp.float32)
        for r in part_refs[1:]:
            s = s + r[0, i].astype(jnp.float32)
        o_ref[...] = s.T.astype(jnp.bfloat16)


def total_heads(first, count, parts, before):
    part = pl.BlockSpec((1, 2, HD, ROWS), lambda h: (h, 0, 0, 0))
    out = pl.BlockSpec((ROWS, HD), lambda h: (0, first + h))
    return pl.pallas_call(
        functools.partial(total, len(parts)),
        grid=(count,),
        in_specs=[part] * len(parts)
        + [pl.BlockSpec(memory_space=pl.ANY)] * len(before),
        out_specs=[out, out],
        out_shape=[jax.ShapeDtypeStruct((ROWS, KVH * HD), jnp.bfloat16)] * 2,
        input_output_aliases={len(parts) + i: i for i in range(len(before))},
        cost_estimate=pl.CostEstimate(
            flops=count * 10 * HD * ROWS,
            bytes_accessed=count * 12 * HD * ROWS * 2,
            transcendentals=0,
        ),
        name="total",
    )(*parts, *before)


def attend_heads(first, count, held, lens, run, wide_args, keys, values, got, before):
    chunks = len(got) + 1
    flops = 12 * count * GROUP * ROWS * HD * chunks * ROWS
    wide = pl.BlockSpec((ROWS, GROUP * HD), lambda h, *_: (0, first + h))
    own = pl.BlockSpec((ROWS, HD), lambda h, *_: (0, first + h))
    skip, width = held
    k_spec = pl.BlockSpec((ROWS, HD), lambda h, *_: (0, skip + h))
    v_spec = pl.BlockSpec((ROWS, HD), lambda h, *_: (0, width + skip + h))
    part = pl.BlockSpec((1, 2, HD, ROWS), lambda h, *_: (h, 0, 0, 0))
    part_shape = jax.ShapeDtypeStruct((count, 2, HD, ROWS), jnp.bfloat16)
    big = jax.ShapeDtypeStruct((ROWS, H * HD), jnp.bfloat16)
    back = chunks - 1
    return pl.pallas_call(
        functools.partial(attend, chunks, len(before)),
        grid_spec=pltpu.PrefetchScalarGridSpec(
            num_scalar_prefetch=2,
            grid=(count,),
            in_specs=[wide, wide]
            + [pl.BlockSpec(memory_space=pl.ANY)] * len(before)
            + [own]
            + [k_spec] * back
            + [own]
            + [v_spec] * back,
            out_specs=[wide, wide] + [part] * chunks,
            scratch_shapes=[pltpu.VMEM((ROWS, chunks * ROWS), jnp.float32)],
        ),
        out_shape=[big, big] + [part_shape] * chunks,
        input_output_aliases={4 + i: i for i in range(len(before))},
        cost_estimate=pl.CostEstimate(
            flops=flops,
            bytes_accessed=4 * count * GROUP * ROWS * HD * 2,
            transcendentals=count * GROUP * ROWS * chunks * ROWS,
        ),
        name="attend",
    )(lens, run, *wide_args, *before, keys, *got, values, *got)


def shift(x, by, n):
    pairs = [(i, i + by) for i in range(n) if 0 <= i + by < n]
    return lax.ppermute(x, "seq", pairs)


def shards(queries, keys, values, lengths, out_grad):
    n = lax.axis_size("seq")
    back = min(n - 1, -(-(MOST - 1) // ROWS))
    chunks = back + 1
    run = lax.axis_index("seq").astype(jnp.int32)[None]
    shifts = list(range(back, 0, -1))
    got = {}
    for first in range(0, KVH, KVH // IN_PIECES):
        count = KVH // IN_PIECES
        cols = slice(first * HD, (first + count) * HD)
        both = jnp.concatenate([keys[:, cols], values[:, cols]], axis=1)
        here = {c: shift(both, c, n) for c in shifts}
        for h in range(first, first + count):
            got[h] = (h - first, count), [here[c] for c in range(1, chunks)]
    before, sums = (), ()
    for first in range(0, KVH, KVH // PIECES):
        count = KVH // PIECES
        held, from_left = got[first]
        att, dq, *own = attend_heads(
            first,
            count,
            held,
            lengths[0],
            run,
            (queries, out_grad),
            keys,
            values,
            from_left,
            before,
        )
        before = att, dq
        sent = [shift(own[c], -c, n) for c in range(1, chunks)]
        sums = total_heads(first, count, own[:1] + sent, sums)
    return (*before, *sums)


def solution(mesh):
    rows = P(("dp", "seq"), None)
    return jax.shard_map(
        shards,
        mesh=mesh,
        in_specs=(rows, rows, rows, P("dp", None), rows),
        out_specs=(rows,) * 4,
        check_vma=False,
    )
```

```python
import functools

import jax
import jax.numpy as jnp
from jax import lax
from jax.experimental import pallas as pl
from jax.experimental.pallas import tpu as pltpu
from jax.sharding import PartitionSpec as P


H = 32
KVH = 4
HD = 128
GROUP = 8
SEGS = 16
MOST = 512
SCALE = HD**-0.5
EXP2_SCALE = SCALE * 1.4426950408889634
NEG = -1e30
ROWS = 128
HEADS_AT_ONCE = 2
SIZES = (1, 2, 3, 4)
VMEM_LIMIT = 48 * 2**20
PIECES = 2
IN_PIECES = 2

NT = (((1,), (1,)), ((), ()))
TN = (((0,), (0,)), ((), ()))


def dot(a, b, dims=(((1,), (0,)), ((), ()))):
    return lax.dot_general(a, b, dims, preferred_element_type=jnp.float32)


def halves(a, b):
    n = a.shape[0] // 2
    return jnp.concatenate([dot(a[:n], b), dot(a[n:], b)], axis=0)


def stack(parts):
    return jnp.concatenate(parts, axis=0)


def attend(chunks, given, held, lens_ref, where_ref, q_ref, g_ref, *refs):
    refs = refs[given:]
    kv_refs = refs[:chunks]
    att_ref, dq_ref = refs[chunks : chunks + 2]
    part_refs = refs[chunks + 2 : 2 * chunks + 2]
    (bias_ref,) = refs[2 * chunks + 2 :]
    run = where_ref[0]
    head, (skip, width) = pl.program_id(0), held

    def at(block, cols=slice(0, HD)):
        return pl.ds(pl.multiple_of(block * HD + cols.start, HD), HD)

    ends = []
    for d in range(SEGS):
        ends.append(lens_ref[d] + (ends[-1] if d else 0))

    @pl.when(pl.program_id(0) == 0)
    def _():
        pos = run * ROWS + lax.broadcasted_iota(jnp.int32, (ROWS, ROWS), 0)
        lane = lax.broadcasted_iota(jnp.int32, (ROWS, ROWS), 1)
        start = jnp.zeros((ROWS, ROWS), jnp.int32)
        for end in ends:
            start = jnp.where(pos >= end, end, start)
        for c in range(chunks):
            key_pos = (run - c) * ROWS + lane
            seen = (key_pos >= start) & (key_pos <= pos)
            bias_ref[:, c * ROWS : (c + 1) * ROWS] = jnp.where(seen, 0.0, NEG)

    oldest = jnp.int32(0)
    for end in ends:
        oldest = jnp.where(run * ROWS >= end, end, oldest)
    live = run - oldest // ROWS + 1

    def work(n):
        k = stack([r[:, at(skip + head)] for r in kv_refs[:n]])
        v = stack([r[:, at(width + skip + head)] for r in kv_refs[:n]])
        v_one = jnp.concatenate([v, jnp.ones((n * ROWS, HD), jnp.bfloat16)], axis=1)
        bias = stack([bias_ref[:, : n * ROWS]] * HEADS_AT_ONCE)
        blocks = range(GROUP // HEADS_AT_ONCE)
        heads = [
            [slice(h * HD, (h + 1) * HD) for h in range(b, b + HEADS_AT_ONCE)]
            for b in range(0, GROUP, HEADS_AT_ONCE)
        ]
        q = [stack([q_ref[:, h] for h in heads[b]]) for b in blocks]
        g = [stack([g_ref[:, h] for h in heads[b]]) for b in blocks]
        expo, weights, g_scaled, rowdot, dscores = ([] for _ in range(5))
        scores = [dot(q[b], k, NT) + bias for b in blocks]
        for b in blocks:
            top = jnp.max(scores[b], axis=1, keepdims=True)
            expo.append(jnp.exp2((scores[b] - top) * EXP2_SCALE))
            weights.append(expo[b].astype(jnp.bfloat16))
        for b in blocks:
            out = halves(weights[b], v_one)
            inv = 1.0 / out[:, HD:]
            att = (out[:, :HD] * inv).astype(jnp.bfloat16)
            wide = g[b].astype(jnp.float32) * inv
            dots = jnp.sum(wide * att.astype(jnp.float32), axis=1, keepdims=True)
            rowdot.append(dots)
            g_scaled.append(wide.astype(jnp.bfloat16))
            for i, h in enumerate(heads[b]):
                att_ref[:, h] = att[i * ROWS : (i + 1) * ROWS]
        for b in blocks:
            dprobs = dot(g_scaled[b], v, NT)
            dscores.append((expo[b] * (dprobs - rowdot[b])).astype(jnp.bfloat16))
        for b in blocks:
            dq = (halves(dscores[b], k) * SCALE).astype(jnp.bfloat16)
            for i, h in enumerate(heads[b]):
                dq_ref[:, h] = dq[i * ROWS : (i + 1) * ROWS]
        dk = dot(stack(q), stack(dscores), TN) * SCALE
        dv = dot(stack(g_scaled), stack(weights), TN)
        for c in range(n):
            cols = slice(c * ROWS, (c + 1) * ROWS)
            part_refs[c][head, 0] = dk[:, cols].astype(jnp.bfloat16)
            part_refs[c][head, 1] = dv[:, cols].astype(jnp.bfloat16)
        for c in range(n, chunks):
            part_refs[c][head] = jnp.zeros_like(part_refs[c][head])

    sizes = [n for n in SIZES if n < chunks] + [chunks]
    for low, n in zip([0] + sizes, sizes):
        pl.when((live > low) & (live <= n))(functools.partial(work, n))


def total(count, *refs):
    part_refs, o_refs = refs[:count], refs[-2:]
    for i, o_ref in enumerate(o_refs):
        for h in range(part_refs[0].shape[0]):
            s = part_refs[0][h, i].astype(jnp.float32)
            for r in part_refs[1:]:
                s = s + r[h, i].astype(jnp.float32)
            o_ref[:, h * HD : (h + 1) * HD] = s.T.astype(jnp.bfloat16)


def total_heads(first, count, parts, before):
    out = pl.BlockSpec((ROWS, count * HD), lambda _: (0, first // count))
    return pl.pallas_call(
        functools.partial(total, len(parts)),
        grid=(1,),
        in_specs=[pl.BlockSpec(memory_space=pltpu.VMEM)] * len(parts)
        + [pl.BlockSpec(memory_space=pl.ANY)] * len(before),
        out_specs=[out, out],
        out_shape=[jax.ShapeDtypeStruct((ROWS, KVH * HD), jnp.bfloat16)] * 2,
        input_output_aliases={len(parts) + i: i for i in range(len(before))},
        cost_estimate=pl.CostEstimate(
            flops=count * 10 * HD * ROWS,
            bytes_accessed=count * 12 * HD * ROWS * 2,
            transcendentals=0,
        ),
        compiler_params=pltpu.CompilerParams(vmem_limit_bytes=VMEM_LIMIT),
        name="total",
    )(*parts, *before)


def attend_heads(first, count, held, lens, run, wide_args, got, before):
    chunks = len(got)
    vmem = pl.BlockSpec(memory_space=pltpu.VMEM)
    wide = pl.BlockSpec((ROWS, GROUP * HD), lambda h, *_: (0, first + h))
    part_shape = jax.ShapeDtypeStruct((count, 2, HD, ROWS), jnp.bfloat16)
    big = jax.ShapeDtypeStruct((ROWS, H * HD), jnp.bfloat16)
    return pl.pallas_call(
        functools.partial(attend, chunks, len(before), held),
        grid_spec=pltpu.PrefetchScalarGridSpec(
            num_scalar_prefetch=2,
            grid=(count,),
            in_specs=[wide, wide]
            + [pl.BlockSpec(memory_space=pl.ANY)] * len(before)
            + [vmem] * chunks,
            out_specs=[wide, wide] + [vmem] * chunks,
            scratch_shapes=[pltpu.VMEM((ROWS, chunks * ROWS), jnp.float32)],
        ),
        out_shape=[big, big] + [part_shape] * chunks,
        input_output_aliases={4 + i: i for i in range(len(before))},
        cost_estimate=pl.CostEstimate(
            flops=12 * count * GROUP * ROWS * HD * chunks * ROWS,
            bytes_accessed=4 * count * GROUP * ROWS * HD * 2,
            transcendentals=count * GROUP * ROWS * chunks * ROWS,
        ),
        compiler_params=pltpu.CompilerParams(vmem_limit_bytes=VMEM_LIMIT),
        name="attend",
    )(lens, run, *wide_args, *before, *got)


def shift(x, by, n):
    pairs = [(i, i + by) for i in range(n) if 0 <= i + by < n]
    return lax.ppermute(x, "seq", pairs)


def shards(queries, keys, values, lengths, out_grad):
    n = lax.axis_size("seq")
    back = min(n - 1, -(-(MOST - 1) // ROWS))
    chunks = back + 1
    run = lax.axis_index("seq").astype(jnp.int32)[None]
    got = {}
    count = KVH // IN_PIECES
    for first in range(0, KVH, count):
        cols = slice(first * HD, (first + count) * HD)
        both = jnp.concatenate([keys[:, cols], values[:, cols]], axis=1)
        here = [shift(both, c, n) for c in range(1, chunks)]
        for h in range(first, first + count):
            got[h] = (h - first, count), [both] + here
    before, sums = (), ()
    for first in range(0, KVH, KVH // PIECES):
        count = KVH // PIECES
        held, runs = got[first]
        att, dq, *own = attend_heads(
            first, count, held, lengths[0], run, (queries, out_grad), runs, before
        )
        before = att, dq
        sent = [shift(own[c], -c, n) for c in range(1, chunks)]
        sums = total_heads(first, count, own[:1] + sent, sums)
    return (*before, *sums)


def solution(mesh):
    rows = P(("dp", "seq"), None)
    return jax.shard_map(
        shards,
        mesh=mesh,
        in_specs=(rows, rows, rows, P("dp", None), rows),
        out_specs=(rows,) * 4,
        check_vma=False,
    )
```

```python
import functools

import jax
import jax.numpy as jnp
from jax import lax
from jax.experimental import pallas as pl
from jax.experimental.pallas import tpu as pltpu
from jax.sharding import PartitionSpec as P


H = 32
KVH = 4
HD = 128
GROUP = 8
SEGS = 16
MOST = 512
SCALE = HD**-0.5
EXP2_SCALE = SCALE * 1.4426950408889634
NEG = -1e30
ROWS = 128
HEADS_AT_ONCE = 2
SIZES = (1, 2, 3, 4)
VMEM_LIMIT = 52 * 2**20
PIECES = ((0, 3), (3, 1))

NT = (((1,), (1,)), ((), ()))
TN = (((0,), (0,)), ((), ()))


def dot(a, b, dims=(((1,), (0,)), ((), ()))):
    return lax.dot_general(a, b, dims, preferred_element_type=jnp.float32)


def halves(a, b):
    n = a.shape[0] // 2
    return jnp.concatenate([dot(a[:n], b), dot(a[n:], b)], axis=0)


def stack(parts):
    return jnp.concatenate(parts, axis=0)


def attend(chunks, given, held, lens_ref, where_ref, q_ref, g_ref, *refs):
    refs = refs[given:]
    kv_refs = refs[:chunks]
    att_ref, dq_ref = refs[chunks : chunks + 2]
    part_refs = refs[chunks + 2 : 2 * chunks + 2]
    (bias_ref,) = refs[2 * chunks + 2 :]
    run = where_ref[0]
    head, (skip, width) = pl.program_id(0), held

    def at(block, cols=slice(0, HD)):
        return pl.ds(pl.multiple_of(block * HD + cols.start, HD), HD)

    ends = []
    for d in range(SEGS):
        ends.append(lens_ref[d] + (ends[-1] if d else 0))

    @pl.when(pl.program_id(0) == 0)
    def _():
        pos = run * ROWS + lax.broadcasted_iota(jnp.int32, (ROWS, ROWS), 0)
        lane = lax.broadcasted_iota(jnp.int32, (ROWS, ROWS), 1)
        start = jnp.zeros((ROWS, ROWS), jnp.int32)
        for end in ends:
            start = jnp.where(pos >= end, end, start)
        for c in range(chunks):
            key_pos = (run - c) * ROWS + lane
            seen = (key_pos >= start) & (key_pos <= pos)
            bias_ref[:, c * ROWS : (c + 1) * ROWS] = jnp.where(seen, 0.0, NEG)

    oldest = jnp.int32(0)
    for end in ends:
        oldest = jnp.where(run * ROWS >= end, end, oldest)
    live = run - oldest // ROWS + 1

    def work(n):
        k = stack([r[:, at(skip + head)] for r in kv_refs[:n]])
        v = stack([r[:, at(width + skip + head)] for r in kv_refs[:n]])
        v_one = jnp.concatenate([v, jnp.ones((n * ROWS, HD), jnp.bfloat16)], axis=1)
        bias = stack([bias_ref[:, : n * ROWS]] * HEADS_AT_ONCE)
        blocks = range(GROUP // HEADS_AT_ONCE)
        heads = [
            [slice(h * HD, (h + 1) * HD) for h in range(b, b + HEADS_AT_ONCE)]
            for b in range(0, GROUP, HEADS_AT_ONCE)
        ]
        q = [stack([q_ref[:, h] for h in heads[b]]) for b in blocks]
        g = [stack([g_ref[:, h] for h in heads[b]]) for b in blocks]
        expo, weights, g_scaled, rowdot, dscores = ([] for _ in range(5))
        scores = [dot(q[b], k, NT) + bias for b in blocks]
        for b in blocks:
            top = jnp.max(scores[b], axis=1, keepdims=True)
            expo.append(jnp.exp2((scores[b] - top) * EXP2_SCALE))
            weights.append(expo[b].astype(jnp.bfloat16))
        for b in blocks:
            out = halves(weights[b], v_one)
            inv = 1.0 / out[:, HD:]
            att = (out[:, :HD] * inv).astype(jnp.bfloat16)
            wide = g[b].astype(jnp.float32) * inv
            dots = jnp.sum(wide * att.astype(jnp.float32), axis=1, keepdims=True)
            rowdot.append(dots)
            g_scaled.append(wide.astype(jnp.bfloat16))
            for i, h in enumerate(heads[b]):
                att_ref[:, h] = att[i * ROWS : (i + 1) * ROWS]
        for b in blocks:
            dprobs = dot(g_scaled[b], v, NT)
            dscores.append((expo[b] * (dprobs - rowdot[b])).astype(jnp.bfloat16))
        for b in blocks:
            dq = (halves(dscores[b], k) * SCALE).astype(jnp.bfloat16)
            for i, h in enumerate(heads[b]):
                dq_ref[:, h] = dq[i * ROWS : (i + 1) * ROWS]
        dk = dot(stack(q), stack(dscores), TN) * SCALE
        dv = dot(stack(g_scaled), stack(weights), TN)
        for c in range(n):
            cols = slice(c * ROWS, (c + 1) * ROWS)
            part_refs[c][head, 0] = dk[:, cols].astype(jnp.bfloat16)
            part_refs[c][head, 1] = dv[:, cols].astype(jnp.bfloat16)
        for c in range(n, chunks):
            part_refs[c][head] = jnp.zeros_like(part_refs[c][head])

    sizes = [n for n in SIZES if n < chunks] + [chunks]
    for low, n in zip([0] + sizes, sizes):
        pl.when((live > low) & (live <= n))(functools.partial(work, n))


def total(count, *refs):
    part_refs, o_refs = refs[:count], refs[-2:]
    for i, o_ref in enumerate(o_refs):
        for h in range(part_refs[0].shape[0]):
            s = part_refs[0][h, i].astype(jnp.float32)
            for r in part_refs[1:]:
                s = s + r[h, i].astype(jnp.float32)
            o_ref[:, h * HD : (h + 1) * HD] = s.T.astype(jnp.bfloat16)


def total_heads(first, count, parts, before):
    out = pl.BlockSpec((ROWS, count * HD), lambda _: (0, first // count))
    return pl.pallas_call(
        functools.partial(total, len(parts)),
        grid=(1,),
        in_specs=[pl.BlockSpec(memory_space=pltpu.VMEM)] * len(parts)
        + [pl.BlockSpec(memory_space=pl.ANY)] * len(before),
        out_specs=[out, out],
        out_shape=[jax.ShapeDtypeStruct((ROWS, KVH * HD), jnp.bfloat16)] * 2,
        input_output_aliases={len(parts) + i: i for i in range(len(before))},
        cost_estimate=pl.CostEstimate(
            flops=count * 10 * HD * ROWS,
            bytes_accessed=count * 12 * HD * ROWS * 2,
            transcendentals=0,
        ),
        compiler_params=pltpu.CompilerParams(vmem_limit_bytes=VMEM_LIMIT),
        name="total",
    )(*parts, *before)


def attend_heads(first, count, held, lens, run, wide_args, got, before):
    chunks = len(got)
    vmem = pl.BlockSpec(memory_space=pltpu.VMEM)
    wide = pl.BlockSpec((ROWS, GROUP * HD), lambda h, *_: (0, first + h))
    part_shape = jax.ShapeDtypeStruct((count, 2, HD, ROWS), jnp.bfloat16)
    big = jax.ShapeDtypeStruct((ROWS, H * HD), jnp.bfloat16)
    return pl.pallas_call(
        functools.partial(attend, chunks, len(before), held),
        grid_spec=pltpu.PrefetchScalarGridSpec(
            num_scalar_prefetch=2,
            grid=(count,),
            in_specs=[wide, wide]
            + [pl.BlockSpec(memory_space=pl.ANY)] * len(before)
            + [vmem] * chunks,
            out_specs=[wide, wide] + [vmem] * chunks,
            scratch_shapes=[pltpu.VMEM((ROWS, chunks * ROWS), jnp.float32)],
        ),
        out_shape=[big, big] + [part_shape] * chunks,
        input_output_aliases={4 + i: i for i in range(len(before))},
        cost_estimate=pl.CostEstimate(
            flops=12 * count * GROUP * ROWS * HD * chunks * ROWS,
            bytes_accessed=4 * count * GROUP * ROWS * HD * 2,
            transcendentals=count * GROUP * ROWS * chunks * ROWS,
        ),
        compiler_params=pltpu.CompilerParams(vmem_limit_bytes=VMEM_LIMIT),
        name="attend",
    )(lens, run, *wide_args, *before, *got)


def shift(x, by, n):
    pairs = [(i, i + by) for i in range(n) if 0 <= i + by < n]
    return lax.ppermute(x, "seq", pairs)


def shards(queries, keys, values, lengths, out_grad):
    n = lax.axis_size("seq")
    back = min(n - 1, -(-(MOST - 1) // ROWS))
    chunks = back + 1
    run = lax.axis_index("seq").astype(jnp.int32)[None]
    got = []
    for first, count in PIECES:
        cols = slice(first * HD, (first + count) * HD)
        both = jnp.concatenate([keys[:, cols], values[:, cols]], axis=1)
        here = [shift(both, c, n) for c in range(1, chunks)]
        got.append([both] + here)
    before, sums = (), ()
    for (first, count), runs in zip(PIECES, got):
        att, dq, *own = attend_heads(
            first, count, (0, count), lengths[0], run, (queries, out_grad), runs, before
        )
        before = att, dq
        sent = [shift(own[c], -c, n) for c in range(1, chunks)]
        sums = total_heads(first, count, own[:1] + sent, sums)
    return (*before, *sums)


def solution(mesh):
    rows = P(("dp", "seq"), None)
    return jax.shard_map(
        shards,
        mesh=mesh,
        in_specs=(rows, rows, rows, P("dp", None), rows),
        out_specs=(rows,) * 4,
        check_vma=False,
    )
```

```python
import functools

import jax
import jax.numpy as jnp
from jax import lax
from jax.experimental import pallas as pl
from jax.experimental.pallas import tpu as pltpu
from jax.sharding import PartitionSpec as P


H = 32
KVH = 4
HD = 128
GROUP = 8
SEGS = 16
MOST = 512
SCALE = HD**-0.5
EXP2_SCALE = SCALE * 1.4426950408889634
NEG = -1e30
ROWS = 128
HEADS_AT_ONCE = 2
SIZES = (1, 2, 3, 4)
VMEM_LIMIT = 52 * 2**20
PIECES = ((0, 3), (3, 1))

NT = (((1,), (1,)), ((), ()))
TN = (((0,), (0,)), ((), ()))


def dot(a, b, dims=(((1,), (0,)), ((), ()))):
    return lax.dot_general(a, b, dims, preferred_element_type=jnp.float32)


def halves(a, b):
    n = a.shape[0] // 2
    return jnp.concatenate([dot(a[:n], b), dot(a[n:], b)], axis=0)


def stack(parts):
    return jnp.concatenate(parts, axis=0)


def attend(chunks, given, held, lens_ref, q_ref, g_ref, *refs):
    refs = refs[given:]
    kv_refs = refs[:chunks]
    att_ref, dq_ref = refs[chunks : chunks + 2]
    part_refs = refs[chunks + 2 : 2 * chunks + 2]
    (bias_ref,) = refs[2 * chunks + 2 :]
    run = lens_ref[SEGS]
    head, (skip, width) = pl.program_id(0), held

    def at(block, cols=slice(0, HD)):
        return pl.ds(pl.multiple_of(block * HD + cols.start, HD), HD)

    ends = []
    for d in range(SEGS):
        ends.append(lens_ref[d] + (ends[-1] if d else 0))

    @pl.when(pl.program_id(0) == 0)
    def _():
        pos = run * ROWS + lax.broadcasted_iota(jnp.int32, (ROWS, ROWS), 0)
        lane = lax.broadcasted_iota(jnp.int32, (ROWS, ROWS), 1)
        start = jnp.zeros((ROWS, ROWS), jnp.int32)
        for end in ends:
            start = jnp.where(pos >= end, end, start)
        for c in range(chunks):
            key_pos = (run - c) * ROWS + lane
            seen = (key_pos >= start) & (key_pos <= pos)
            bias_ref[:, c * ROWS : (c + 1) * ROWS] = jnp.where(seen, 0.0, NEG)

    oldest = jnp.int32(0)
    for end in ends:
        oldest = jnp.where(run * ROWS >= end, end, oldest)
    live = run - oldest // ROWS + 1

    def work(n):
        k = stack([r[:, at(skip + head)] for r in kv_refs[:n]])
        v = stack([r[:, at(width + skip + head)] for r in kv_refs[:n]])
        v_one = jnp.concatenate([v, jnp.ones((n * ROWS, HD), jnp.bfloat16)], axis=1)
        bias = stack([bias_ref[:, : n * ROWS]] * HEADS_AT_ONCE)
        blocks = range(GROUP // HEADS_AT_ONCE)
        heads = [
            [slice(h * HD, (h + 1) * HD) for h in range(b, b + HEADS_AT_ONCE)]
            for b in range(0, GROUP, HEADS_AT_ONCE)
        ]
        q = [stack([q_ref[:, h] for h in heads[b]]) for b in blocks]
        g = [stack([g_ref[:, h] for h in heads[b]]) for b in blocks]
        expo, weights, g_scaled, rowdot, dscores = ([] for _ in range(5))
        scores = [dot(q[b], k, NT) + bias for b in blocks]
        for b in blocks:
            top = jnp.max(scores[b], axis=1, keepdims=True)
            expo.append(jnp.exp2((scores[b] - top) * EXP2_SCALE))
            weights.append(expo[b].astype(jnp.bfloat16))
        for b in blocks:
            out = halves(weights[b], v_one)
            inv = 1.0 / out[:, HD:]
            att = (out[:, :HD] * inv).astype(jnp.bfloat16)
            wide = g[b].astype(jnp.float32) * inv
            dots = jnp.sum(wide * att.astype(jnp.float32), axis=1, keepdims=True)
            rowdot.append(dots)
            g_scaled.append(wide.astype(jnp.bfloat16))
            for i, h in enumerate(heads[b]):
                att_ref[:, h] = att[i * ROWS : (i + 1) * ROWS]
        for b in blocks:
            dprobs = dot(g_scaled[b], v, NT)
            dscores.append((expo[b] * (dprobs - rowdot[b])).astype(jnp.bfloat16))
        for b in blocks:
            dq = (halves(dscores[b], k) * SCALE).astype(jnp.bfloat16)
            for i, h in enumerate(heads[b]):
                dq_ref[:, h] = dq[i * ROWS : (i + 1) * ROWS]
        dk = dot(stack(q), stack(dscores), TN) * SCALE
        dv = dot(stack(g_scaled), stack(weights), TN)
        for c in range(n):
            cols = slice(c * ROWS, (c + 1) * ROWS)
            part_refs[c][head, 0] = dk[:, cols].astype(jnp.bfloat16)
            part_refs[c][head, 1] = dv[:, cols].astype(jnp.bfloat16)
        for c in range(n, chunks):
            part_refs[c][head] = jnp.zeros_like(part_refs[c][head])

    sizes = [n for n in SIZES if n < chunks] + [chunks]
    for low, n in zip([0] + sizes, sizes):
        pl.when((live > low) & (live <= n))(functools.partial(work, n))


def total(count, *refs):
    part_refs, o_refs = refs[:count], refs[-2:]
    for i, o_ref in enumerate(o_refs):
        for h in range(part_refs[0].shape[0]):
            s = part_refs[0][h, i].astype(jnp.float32)
            for r in part_refs[1:]:
                s = s + r[h, i].astype(jnp.float32)
            o_ref[:, h * HD : (h + 1) * HD] = s.T.astype(jnp.bfloat16)


def total_heads(first, count, parts, before):
    out = pl.BlockSpec((ROWS, count * HD), lambda _: (0, first // count))
    return pl.pallas_call(
        functools.partial(total, len(parts)),
        grid=(1,),
        in_specs=[pl.BlockSpec(memory_space=pltpu.VMEM)] * len(parts)
        + [pl.BlockSpec(memory_space=pl.ANY)] * len(before),
        out_specs=[out, out],
        out_shape=[jax.ShapeDtypeStruct((ROWS, KVH * HD), jnp.bfloat16)] * 2,
        input_output_aliases={len(parts) + i: i for i in range(len(before))},
        cost_estimate=pl.CostEstimate(
            flops=count * 10 * HD * ROWS,
            bytes_accessed=count * 12 * HD * ROWS * 2,
            transcendentals=0,
        ),
        compiler_params=pltpu.CompilerParams(vmem_limit_bytes=VMEM_LIMIT),
        name="total",
    )(*parts, *before)


def attend_heads(first, count, held, facts, wide_args, got, before):
    chunks = len(got)
    vmem = pl.BlockSpec(memory_space=pltpu.VMEM)
    wide = pl.BlockSpec((ROWS, GROUP * HD), lambda h, *_: (0, first + h))
    part_shape = jax.ShapeDtypeStruct((count, 2, HD, ROWS), jnp.bfloat16)
    big = jax.ShapeDtypeStruct((ROWS, H * HD), jnp.bfloat16)
    return pl.pallas_call(
        functools.partial(attend, chunks, len(before), held),
        grid_spec=pltpu.PrefetchScalarGridSpec(
            num_scalar_prefetch=1,
            grid=(count,),
            in_specs=[wide, wide]
            + [pl.BlockSpec(memory_space=pl.ANY)] * len(before)
            + [vmem] * chunks,
            out_specs=[wide, wide] + [vmem] * chunks,
            scratch_shapes=[pltpu.VMEM((ROWS, chunks * ROWS), jnp.float32)],
        ),
        out_shape=[big, big] + [part_shape] * chunks,
        input_output_aliases={3 + i: i for i in range(len(before))},
        cost_estimate=pl.CostEstimate(
            flops=12 * count * GROUP * ROWS * HD * chunks * ROWS,
            bytes_accessed=4 * count * GROUP * ROWS * HD * 2,
            transcendentals=count * GROUP * ROWS * chunks * ROWS,
        ),
        compiler_params=pltpu.CompilerParams(vmem_limit_bytes=VMEM_LIMIT),
        name="attend",
    )(facts, *wide_args, *before, *got)


def shift(x, by, n):
    pairs = [(i, i + by) for i in range(n) if 0 <= i + by < n]
    return lax.ppermute(x, "seq", pairs)


def shards(queries, keys, values, lengths, out_grad):
    n = lax.axis_size("seq")
    back = min(n - 1, -(-(MOST - 1) // ROWS))
    chunks = back + 1
    run = lax.axis_index("seq").astype(jnp.int32)[None]
    facts = jnp.concatenate([lengths[0], run])
    got = []
    for first, count in PIECES:
        cols = slice(first * HD, (first + count) * HD)
        both = jnp.concatenate([keys[:, cols], values[:, cols]], axis=1)
        here = [shift(both, c, n) for c in range(1, chunks)]
        got.append([both] + here)
    before, sums = (), ()
    for (first, count), runs in zip(PIECES, got):
        att, dq, *own = attend_heads(
            first, count, (0, count), facts, (queries, out_grad), runs, before
        )
        before = att, dq
        sent = [shift(own[c], -c, n) for c in range(1, chunks)]
        sums = total_heads(first, count, own[:1] + sent, sums)
    return (*before, *sums)


def solution(mesh):
    rows = P(("dp", "seq"), None)
    return jax.shard_map(
        shards,
        mesh=mesh,
        in_specs=(rows, rows, rows, P("dp", None), rows),
        out_specs=(rows,) * 4,
        check_vma=False,
    )
```
